32 devices in a mesh: seq: 8 (over y, x, core), sub: 4 (over z).
Axes of the slice: x: 2, y: 2, z: 4, core: 2. Of those that a mesh axis runs over, the one named last changes fastest.
Arguments:
- query_rows: bfloat16 [8192, 1120], P(('seq', 'sub')), may hold values from -6 to 6
- key_rows: bfloat16 [8192, 1120], P(('seq', 'sub')), may hold values from -6 to 6
- value_rows: bfloat16 [8192, 1120], P(('seq', 'sub')), may hold values from -6 to 6
- query_tangent: bfloat16 [8192, 1120], P(('seq', 'sub')), may hold values from -6 to 6
- key_tangent: bfloat16 [8192, 1120], P(('seq', 'sub')), may hold values from -6 to 6
- value_tangent: bfloat16 [8192, 1120], P(('seq', 'sub')), may hold values from -6 to 6
- teacher: bfloat16 [8192, 2240], P(('seq', 'sub')), may hold values from -64 to 64
- out_weight: bfloat16 [1120, 2240], replicated, may hold values from -0.1875 to 0.1875
- norm_gain: float32 [1120], replicated, may hold values from 0.1 to 1.9
- clip_length: int32 [1], replicated, may hold values from 4096 to 8192
- block_mask: int32 [128], P(('seq', 'sub')), may hold values 0 or 1
Outputs:
- residual: bfloat16 [8192, 2240], P(('seq', 'sub'))
- grad_query: bfloat16 [8192, 1120], P(('seq', 'sub'))
- grad_key: bfloat16 [8192, 1120], P(('seq', 'sub'))
- grad_value: bfloat16 [8192, 1120], P(('seq', 'sub'))
The draws below stay inside these ranges and needn't reach their ends.
All inputs are finite; a program needn't handle non-finite values. No bound on the sum of `block_mask` on one device may be relied on, other than what follows from the above.
Results may differ from the reference program's by a relative error of at most 0.007.
Values may be sent and summed in bfloat16 or wider, within the bound.
A program may use at most 64 MiB of HBM per device.

```python
import jax
import jax.numpy as jnp
from jax import lax

D = 2240
H = 10
E = 112
BLK = 64
TOKENS = 8192
NBLK = 128


def draw_teacher(key, part):
    level_key = jax.random.fold_in(key, 11)
    entry_key = jax.random.fold_in(key, 12)
    groups = (TOKENS + 255) // 256
    levels = 6.0 * jnp.exp(jax.random.uniform(level_key, (groups,), jnp.float32, -1.0, 1.0))
    entries = jnp.clip(jax.random.normal(entry_key, (TOKENS, D), jnp.float32), -3.5, 3.5)
    row_group = jnp.arange(TOKENS, dtype=jnp.int32) // 256
    return (levels[row_group][:, None] * entries).astype(jnp.bfloat16)


def touch_ends(drawn, stream_key, low, largest):
    spot = [jax.random.randint(jax.random.fold_in(stream_key, axis), (), 0, length) for axis, length in enumerate(drawn.shape)]
    longest = drawn.shape.index(max(drawn.shape))
    next_to = spot[:longest] + [(spot[longest] + 1) % drawn.shape[longest]] + spot[longest + 1:]
    return drawn.at[tuple(spot)].set(low).at[tuple(next_to)].set(largest)


def block_levels(own_key, shape, split, least, largest):
    def one(axis_at, parts):
        steps = jax.random.uniform(jax.random.fold_in(jax.random.fold_in(own_key, 6), axis_at), (parts,), jnp.float32, least / len(split), largest / len(split))
        return jnp.repeat(jnp.exp(steps), shape[axis_at] // parts).reshape((-1,) + (1,) * (len(shape) - axis_at - 1))

    gain = one(*split[0])
    for cut in split[1:]:
        gain = gain * one(*cut)
    return gain


def normal_values(key, extent, spread, reach, cuts=(), kind=jnp.bfloat16):
    factor_of = block_levels(key, extent, cuts, -0.22, 0.18) if cuts else 1.0
    values = jax.random.normal(key, extent, jnp.float32) * spread * factor_of
    return jnp.minimum(jnp.maximum(values, -reach), reach).astype(kind)


def setup_inputs(seed: int = 0) -> dict:
    key_of = jax.random.split(jax.random.key(seed), 12)
    query_rows = normal_values(key_of[0], (TOKENS, H * E), 1.0, 6.0, ((0, 32),))
    key_rows = normal_values(key_of[1], (TOKENS, H * E), 1.0, 6.0, ((0, 32),))
    value_rows = normal_values(key_of[2], (TOKENS, H * E), 1.0, 6.0, ((0, 32),))
    query_tangent = normal_values(key_of[3], (TOKENS, H * E), 1.0, 6.0, ((0, 32),))
    key_tangent = normal_values(key_of[4], (TOKENS, H * E), 1.0, 6.0, ((0, 32),))
    value_tangent = normal_values(key_of[5], (TOKENS, H * E), 1.0, 6.0, ((0, 32),))
    teacher = draw_teacher(jax.random.fold_in(key_of[11], 71), 0)
    out_weight = normal_values(key_of[7], (H * E, D), (H * E) ** -0.5, 0.1875)
    norm_gain = jnp.clip(1.0 + 0.18 * jax.random.normal(key_of[8], (H * E,), jnp.float32), 0.1, 1.9)
    clip_length = jax.random.randint(key_of[9], (1,), TOKENS // 2, TOKENS + 1).astype(jnp.int32)
    block_mask = touch_ends((jax.random.randint(key_of[10], (NBLK,), 0, 8) < 7).astype(jnp.int32), jax.random.fold_in(key_of[10], 1), 0, 1)
    return dict(query_rows=query_rows, key_rows=key_rows, value_rows=value_rows, query_tangent=query_tangent, key_tangent=key_tangent, value_tangent=value_tangent, teacher=teacher, out_weight=out_weight, norm_gain=norm_gain, clip_length=clip_length, block_mask=block_mask)


def split_heads(matrix):
    return matrix.reshape(matrix.shape[0], H, E)

def norm_back(unnorm, scale_inv, weighted):
    inner_mean = lax.optimization_barrier(jnp.mean(unnorm * weighted, axis=-1, keepdims=True))
    return scale_inv * weighted - unnorm * (scale_inv * scale_inv * scale_inv) * inner_mean

def reference(query_rows, key_rows, value_rows, query_tangent, key_tangent, value_tangent, teacher, out_weight, norm_gain, clip_length, block_mask):
    f32 = jnp.float32
    bf16 = jnp.bfloat16
    seq_total = query_rows.shape[0]
    position = jnp.arange(seq_total, dtype=jnp.int32)
    block_flags = jnp.repeat(block_mask, BLK)
    valid_rows = jnp.where((position < clip_length[0]) & (block_flags == 1), 1.0, 0.0).astype(f32)[:, None]
    key_vals = key_rows.astype(f32)
    key_feat = (valid_rows * jnp.maximum(key_vals, 0.0)).astype(bf16)
    key_slope = valid_rows * jnp.where(key_vals > 0, 1.0, 0.0).astype(f32)
    key_dot = (key_slope * key_tangent.astype(f32)).astype(bf16)
    value_heads = split_heads(value_rows).astype(f32)
    feat_keys = split_heads(key_feat).astype(f32)
    state = jnp.einsum('the,thf->hef', feat_keys, value_heads).astype(bf16)
    state_dot = (jnp.einsum('the,thf->hef', split_heads(key_dot).astype(f32), value_heads) + jnp.einsum('the,thf->hef', feat_keys, split_heads(value_tangent).astype(f32))).astype(bf16)
    query_vals = query_rows.astype(f32)
    query_feat = jnp.maximum(query_vals, 0.0).astype(bf16)
    query_slope = jnp.where(query_vals > 0, 1.0, 0.0).astype(f32)
    query_dot = (query_slope * query_tangent.astype(f32)).astype(bf16)
    feat_heads = split_heads(query_feat).astype(f32)
    state_full = state.astype(f32)
    unnorm = jnp.einsum('the,hef->thf', feat_heads, state_full)
    unnorm_dot = jnp.einsum('the,hef->thf', split_heads(query_dot).astype(f32), state_full) + jnp.einsum('the,hef->thf', feat_heads, state_dot.astype(f32))
    gain_heads = norm_gain.reshape(H, E)
    scale_inv = lax.rsqrt(lax.optimization_barrier(jnp.mean(unnorm * unnorm, axis=-1, keepdims=True)) + 1e-06)
    normed_dot = (gain_heads * norm_back(unnorm, scale_inv, unnorm_dot)).astype(bf16).reshape(seq_total, H * E)
    velocity = jnp.dot(normed_dot, out_weight, preferred_element_type=f32)
    residual = (velocity - teacher.astype(f32)).astype(bf16)
    normed_grad = jnp.dot(residual, out_weight.T, preferred_element_type=f32)
    unnorm_grad = norm_back(unnorm, scale_inv, gain_heads * split_heads(normed_grad)).astype(bf16)
    grad_heads = unnorm_grad.astype(f32)
    state_grad = jnp.einsum('the,thf->hef', feat_heads, grad_heads).astype(bf16).astype(f32)
    grad_query = (query_slope * jnp.einsum('thf,hef->the', grad_heads, state_full).reshape(seq_total, H * E)).astype(bf16)
    grad_key = (key_slope * jnp.einsum('thf,hef->the', value_heads, state_grad).reshape(seq_total, H * E)).astype(bf16)
    grad_value = jnp.einsum('the,hef->thf', feat_keys, state_grad).reshape(seq_total, H * E).astype(bf16)
    return (residual, grad_query, grad_key, grad_value)
```

```python
import functools

import jax
import jax.numpy as jnp
from jax import lax
from jax.experimental import pallas as pl
from jax.experimental.pallas import tpu as pltpu
from jax.sharding import PartitionSpec as P

H = 10
E = 112
BLK = 64


def split_heads(matrix):
    return matrix.reshape(matrix.shape[0], H, E)


def norm_back(unnorm, scale_inv, weighted):
    inner_mean = jnp.mean(unnorm * weighted, axis=-1, keepdims=True)
    return scale_inv * weighted - unnorm * (scale_inv * scale_inv * scale_inv) * inner_mean


MESH = pl.DeviceIdType.MESH


def total_kernel(
    outer, x_ref, out_ref, half, mine, parts, s0, r0, s1, r1, s2, r2, s3, r3
):
    seq = lax.axis_index("seq")
    sub = lax.axis_index("sub")
    depth = lax.axis_size("sub")
    chips = outer
    core = lax.rem(seq, 2)
    chip = (seq // 2) * depth + sub
    partner = (seq + 1 - 2 * core, sub)

    def peer(index):
        return (index // depth) * 2 + core, lax.rem(index, depth)

    def ahead(step):
        return lax.rem(chip + step, chips)

    def behind(step):
        return lax.rem(chip + chips - step, chips)

    barrier = pltpu.get_barrier_semaphore()
    pl.semaphore_signal(barrier, inc=1, device_id=partner, device_id_type=MESH)

    @pl.loop(1, chips)
    def _(step):
        pl.semaphore_signal(barrier, inc=1, device_id=peer(ahead(step)), device_id_type=MESH)

    pl.semaphore_wait(barrier, chips)

    swap = pltpu.make_async_remote_copy(
        src_ref=x_ref.at[1 - core],
        dst_ref=half,
        send_sem=s0,
        recv_sem=r0,
        device_id=partner,
        device_id_type=MESH,
    )
    swap.start()
    swap.wait()

    def scatter(index):
        return pltpu.make_async_remote_copy(
            src_ref=mine.at[index],
            dst_ref=parts.at[chip],
            send_sem=s1.at[index],
            recv_sem=r1.at[chip],
            device_id=peer(index),
            device_id_type=MESH,
        )

    def scattered(index):
        return pltpu.make_async_remote_copy(
            src_ref=mine.at[index],
            dst_ref=parts.at[index],
            send_sem=s1.at[index],
            recv_sem=r1.at[index],
            device_id=peer(index),
            device_id_type=MESH,
        )

    def pair(index):
        return x_ref[core, index].astype(jnp.float32) + half[index].astype(jnp.float32)

    @pl.loop(1, chips)
    def _(step):
        index = ahead(step)
        mine[index] = pair(index).astype(mine.dtype)
        scatter(index).start()

    def add(step, acc):
        index = behind(step)
        scattered(index).wait_recv()
        return acc + parts[index].astype(jnp.float32)

    total = lax.fori_loop(1, chips, add, pair(chip))
    out_ref[core, chip] = total.astype(out_ref.dtype)

    def gather(index):
        return pltpu.make_async_remote_copy(
            src_ref=out_ref.at[core, chip],
            dst_ref=out_ref.at[core, chip],
            send_sem=s2.at[index],
            recv_sem=r2.at[chip],
            device_id=peer(index),
            device_id_type=MESH,
        )

    def gathered(index):
        return pltpu.make_async_remote_copy(
            src_ref=out_ref.at[core, chip],
            dst_ref=out_ref.at[core, index],
            send_sem=s2.at[index],
            recv_sem=r2.at[index],
            device_id=peer(index),
            device_id_type=MESH,
        )

    def forward(index):
        return pltpu.make_async_remote_copy(
            src_ref=out_ref.at[core, index],
            dst_ref=out_ref.at[core, index],
            send_sem=s3.at[index],
            recv_sem=r3.at[index],
            device_id=partner,
            device_id_type=MESH,
        )

    def forwarded(index):
        return pltpu.make_async_remote_copy(
            src_ref=out_ref.at[core, index],
            dst_ref=out_ref.at[1 - core, index],
            send_sem=s3.at[index],
            recv_sem=r3.at[index],
            device_id=partner,
            device_id_type=MESH,
        )

    @pl.loop(1, chips)
    def _(step):
        gather(ahead(step)).start()

    forward(chip).start()

    @pl.loop(1, chips)
    def _(step):
        index = behind(step)
        gathered(index).wait_recv()
        forward(index).start()

    @pl.loop(1, chips)
    def _(step):
        index = ahead(step)
        scatter(index).wait_send()
        gather(index).wait_send()

    @pl.loop(0, chips)
    def _(step):
        index = behind(step)
        forwarded(index).wait_recv()
        forward(index).wait_send()


def combine_states(stacked, collective_id):
    mats, rows, cols = stacked.shape
    chips = lax.axis_size("seq") // 2 * lax.axis_size("sub")
    piece = -(-(mats * rows) // (32 * chips)) * 16
    flat = stacked.reshape(mats * rows, cols).astype(jnp.bfloat16)
    flat = jnp.pad(flat, ((0, 2 * chips * piece - mats * rows), (0, 0)))
    grid = flat.reshape(2, chips, piece, cols)
    dma = pltpu.SemaphoreType.DMA
    totals = pl.pallas_call(
        functools.partial(total_kernel, chips),
        out_shape=jax.ShapeDtypeStruct(grid.shape, jnp.bfloat16),
        in_specs=[pl.BlockSpec(memory_space=pltpu.VMEM)],
        out_specs=pl.BlockSpec(memory_space=pltpu.VMEM),
        scratch_shapes=[pltpu.VMEM(grid.shape[1:], jnp.bfloat16)] * 3
        + [dma, dma]
        + [dma((chips,))] * 6,
        compiler_params=pltpu.CompilerParams(collective_id=collective_id, has_side_effects=True),
    )(grid)
    return totals.reshape(2 * chips * piece, cols)[: mats * rows].reshape(mats, rows, cols)


def local(
    query_rows,
    key_rows,
    value_rows,
    query_tangent,
    key_tangent,
    value_tangent,
    teacher,
    out_weight,
    norm_gain,
    clip_length,
    block_mask,
):
    f32 = jnp.float32
    bf16 = jnp.bfloat16
    tok_rows = query_rows.shape[0]
    first_row = (lax.axis_index("seq") * lax.axis_size("sub") + lax.axis_index("sub")) * tok_rows
    position = first_row + lax.iota(jnp.int32, tok_rows)
    block_flags = jnp.broadcast_to(block_mask[:, None], (tok_rows // BLK, BLK)).reshape(tok_rows)
    valid_rows = jnp.where((position < clip_length[0]) & (block_flags == 1), 1.0, 0.0).astype(f32)[
        :, None
    ]
    key_vals = key_rows.astype(f32)
    key_feat = (valid_rows * jnp.maximum(key_vals, 0.0)).astype(bf16)
    key_slope = valid_rows * jnp.where(key_vals > 0, 1.0, 0.0).astype(f32)
    key_dot = (key_slope * key_tangent.astype(f32)).astype(bf16)
    value_heads = split_heads(value_rows)
    feat_keys = split_heads(key_feat)
    state_part = jnp.einsum("the,thf->hef", feat_keys, value_heads, preferred_element_type=f32)
    tangent_part = jnp.einsum(
        "the,thf->hef", split_heads(key_dot), value_heads, preferred_element_type=f32
    ) + jnp.einsum(
        "the,thf->hef", feat_keys, split_heads(value_tangent), preferred_element_type=f32
    )
    states = combine_states(jnp.concatenate([state_part, tangent_part]), 0)
    state = states[:H]
    state_dot = states[H:]
    query_vals = query_rows.astype(f32)
    query_feat = jnp.maximum(query_vals, 0.0).astype(bf16)
    query_slope = jnp.where(query_vals > 0, 1.0, 0.0).astype(f32)
    query_dot = (query_slope * query_tangent.astype(f32)).astype(bf16)
    feat_heads = split_heads(query_feat)
    unnorm = jnp.einsum("the,hef->thf", feat_heads, state, preferred_element_type=f32)
    unnorm_dot = jnp.einsum(
        "the,hef->thf", split_heads(query_dot), state, preferred_element_type=f32
    ) + jnp.einsum("the,hef->thf", feat_heads, state_dot, preferred_element_type=f32)
    gain_heads = norm_gain.reshape(H, E)
    scale_inv = lax.rsqrt(jnp.mean(unnorm * unnorm, axis=-1, keepdims=True) + 1e-06)
    normed_dot = (
        (gain_heads * norm_back(unnorm, scale_inv, unnorm_dot))
        .astype(bf16)
        .reshape(tok_rows, H * E)
    )
    velocity = jnp.dot(normed_dot, out_weight, preferred_element_type=f32)
    residual = (velocity - teacher.astype(f32)).astype(bf16)
    normed_grad = lax.dot_general(
        residual, out_weight, (((1,), (1,)), ((), ())), preferred_element_type=f32
    )
    unnorm_grad = norm_back(unnorm, scale_inv, gain_heads * split_heads(normed_grad)).astype(bf16)
    grad_part = jnp.einsum("the,thf->hef", feat_heads, unnorm_grad, preferred_element_type=f32)
    state_grad = combine_states(grad_part, 1)
    grad_query = (
        query_slope
        * jnp.einsum("thf,hef->the", unnorm_grad, state, preferred_element_type=f32).reshape(
            tok_rows, H * E
        )
    ).astype(bf16)
    grad_key = (
        key_slope
        * jnp.einsum("thf,hef->the", value_heads, state_grad, preferred_element_type=f32).reshape(
            tok_rows, H * E
        )
    ).astype(bf16)
    grad_value = (
        jnp.einsum("the,hef->thf", feat_keys, state_grad, preferred_element_type=f32)
        .reshape(tok_rows, H * E)
        .astype(bf16)
    )
    return (residual, grad_query, grad_key, grad_value)


def solution(mesh):
    return jax.shard_map(
        local,
        mesh=mesh,
        in_specs=(
            P(("seq", "sub"), None),
            P(("seq", "sub"), None),
            P(("seq", "sub"), None),
            P(("seq", "sub"), None),
            P(("seq", "sub"), None),
            P(("seq", "sub"), None),
            P(("seq", "sub"), None),
            P(),
            P(),
            P(),
            P(("seq", "sub")),
        ),
        out_specs=(
            P(("seq", "sub"), None),
            P(("seq", "sub"), None),
            P(("seq", "sub"), None),
            P(("seq", "sub"), None),
        ),
        check_vma=False,
    )
```

```python
import functools

import jax
import jax.numpy as jnp
from jax import lax
from jax.experimental import pallas as pl
from jax.experimental.pallas import tpu as pltpu
from jax.sharding import PartitionSpec as P

H = 10
E = 112
BLK = 64


MESH = pl.DeviceIdType.MESH
LANES = 128
f32 = jnp.float32
bf16 = jnp.bfloat16


def norm_back(unnorm, scale_inv, weighted):
    inner_mean = jnp.mean(unnorm * weighted, axis=-1, keepdims=True)
    return scale_inv * weighted - unnorm * (scale_inv * scale_inv * scale_inv) * inner_mean


def dot(left, right, over):
    return lax.dot_general(left, right, ((over[:1], over[1:]), ((), ())), preferred_element_type=f32)


class Where:
    def __init__(self, chips, depth):
        seq = lax.axis_index("seq")
        self.sub = lax.axis_index("sub")
        self.depth = depth
        self.chips = chips
        self.core = lax.rem(seq, 2)
        self.chip = (seq // 2) * depth + self.sub
        self.partner = (seq + 1 - 2 * self.core, self.sub)

    def peer(self, index):
        return (index // self.depth) * 2 + self.core, lax.rem(index, self.depth)

    def ahead(self, step):
        return lax.rem(self.chip + step, self.chips)

    def behind(self, step):
        return lax.rem(self.chip + self.chips - step, self.chips)


def greet(at):
    barrier = pltpu.get_barrier_semaphore()
    pl.semaphore_signal(barrier, inc=1, device_id=at.partner, device_id_type=MESH)

    @pl.loop(1, at.chips)
    def _(step):
        pl.semaphore_signal(
            barrier, inc=1, device_id=at.peer(at.ahead(step)), device_id_type=MESH
        )


def all_total(at, piece, wide, near, sent, out, half, mine, parts, sems, between=None):
    s0, r0, s1, r1, s2, r2, s3, r3 = sems
    core, chip, chips = at.core, at.chip, at.chips

    def copy(src, dst, send, recv, to):
        return pltpu.make_async_remote_copy(
            src_ref=src,
            dst_ref=dst,
            send_sem=send,
            recv_sem=recv,
            device_id=to,
            device_id_type=MESH,
        )

    def rows(index, side=None):
        base = index if side is None else side * chips + index
        return pl.ds(pl.multiple_of(base * piece, 16), piece)

    def scatter(index, slot):
        return copy(
            mine.at[rows(index)], parts.at[rows(slot)], s1.at[index], r1.at[slot], at.peer(index)
        )

    def gather(index, slot):
        return copy(
            out.at[rows(chip, core)],
            out.at[rows(slot, core)],
            s2.at[index],
            r2.at[slot],
            at.peer(index),
        )

    def forward(index, side):
        return copy(
            out.at[rows(index, core)],
            out.at[rows(index, side)],
            s3.at[index],
            r3.at[index],
            at.partner,
        )

    size = wide.shape[0]
    for block in range(wide.shape[1] // LANES):
        lanes = wide[:, block * LANES : (block + 1) * LANES]
        near[block * size : (block + 1) * size, :] = lanes
        sent[block * size : (block + 1) * size, :] = lanes.astype(bf16)
    used = size * (wide.shape[1] // LANES)
    if used < near.shape[0]:
        near[used:, :] = jnp.zeros((near.shape[0] - used, LANES), f32)
        sent[used:, :] = jnp.zeros((near.shape[0] - used, LANES), bf16)

    other = pl.ds(pl.multiple_of((1 - core) * (chips * piece), 16), chips * piece)
    swap = copy(sent.at[other], half, s0, r0, at.partner)
    swap.start()
    if between is not None:
        between()
    swap.wait()

    def pair(index):
        return near[rows(index, core), :] + half[rows(index), :].astype(f32)

    @pl.loop(1, chips)
    def _(step):
        index = at.ahead(step)
        mine[rows(index), :] = pair(index).astype(bf16)
        scatter(index, chip).start()

    def add(step, acc):
        index = at.behind(step)
        scatter(index, index).wait_recv()
        return acc + parts[rows(index), :].astype(f32)

    out[rows(chip, core), :] = lax.fori_loop(1, chips, add, pair(chip)).astype(bf16)

    @pl.loop(1, chips)
    def _(step):
        gather(at.ahead(step), chip).start()

    forward(chip, core).start()

    @pl.loop(1, chips)
    def _(step):
        index = at.behind(step)
        gather(index, index).wait_recv()
        forward(index, core).start()

    @pl.loop(1, chips)
    def _(step):
        index = at.ahead(step)
        scatter(index, chip).wait_send()
        gather(index, chip).wait_send()

    @pl.loop(0, chips)
    def _(step):
        index = at.behind(step)
        forward(index, 1 - core).wait_recv()
        forward(index, core).wait_send()

    for block in range(wide.shape[1] // LANES):
        wide[:, block * LANES : (block + 1) * LANES] = out[
            block * size : (block + 1) * size, :
        ].astype(f32)


def step_kernel(
    chips, depth, pieces,
    q_hbm, k_hbm, v_hbm, qt_hbm, kt_hbm, vt_hbm, t_hbm, w_hbm, gain_ref, clip_ref, flags_ref,
    res_ref, gq_ref, gk_ref, gv_ref,
    q, k, v, qt, kt, vt, teach, weight, loads,
    wide1, near1, sent1, out1, half1, mine1, parts1,
    wide2, near2, sent2, out2, half2, mine2, parts2,
    unnorm, scale, normed, ngrad, ugrad,
    *sems,
):
    at = Where(chips, depth)
    tok = q.shape[0]
    incoming = [
        pltpu.make_async_copy(src, dst, loads.at[i])
        for i, (src, dst) in enumerate(
            [
                (k_hbm, k),
                (v_hbm, v),
                (kt_hbm, kt),
                (vt_hbm, vt),
                (q_hbm, q),
                (qt_hbm, qt),
                (w_hbm, weight),
                (t_hbm, teach),
            ]
        )
    ]
    greet(at)
    for load in incoming:
        load.start()

    rowid = lax.broadcasted_iota(jnp.int32, (tok, E), 0)
    device = lax.axis_index("seq") * depth + at.sub
    kept = jnp.zeros((tok, E), jnp.int32)
    for block in range(tok // BLK):
        inside = (rowid >= block * BLK) & (rowid < (block + 1) * BLK)
        kept = jnp.where(inside, flags_ref[block], kept)
    before = rowid + device * tok < clip_ref[0]
    valid = jnp.where(before & (kept == 1), 1.0, 0.0).astype(f32)

    def head(ref, h):
        return ref[:, h * E : (h + 1) * E]

    def key_parts(h):
        keys = head(k, h).astype(f32)
        slope = jnp.where(keys > 0, valid, 0.0)
        return jnp.maximum(keys, 0.0) * valid, slope

    for load in incoming[:4]:
        load.wait()
    edge = wide1.shape[1] - LANES
    wide1[:, edge:] = jnp.zeros((wide1.shape[0], LANES), f32)
    wide2[:, edge:] = jnp.zeros((wide2.shape[0], LANES), f32)
    for h in range(H):
        feat, slope = key_parts(h)
        feat = feat.astype(bf16)
        along = (slope * head(kt, h).astype(f32)).astype(bf16)
        vals = head(v, h)
        cols = slice(h * E, (h + 1) * E)
        wide1[:E, cols] = dot(feat, vals, (0, 0))
        wide1[E:, cols] = dot(along, vals, (0, 0)) + dot(feat, head(vt, h), (0, 0))

    pl.semaphore_wait(pltpu.get_barrier_semaphore(), chips)
    all_total(
        at, pieces[0], wide1, near1, sent1, out1, half1, mine1, parts1, sems[:8]
    )

    for load in incoming[4:]:
        load.wait()

    def state(h):
        return head(wide1, h)[:E].astype(bf16)

    def query(h):
        rows = head(q, h).astype(f32)
        return jnp.maximum(rows, 0.0).astype(bf16), jnp.where(rows > 0, 1.0, 0.0).astype(f32)

    for h in range(H):
        both = head(wide1, h).astype(bf16)
        feat, slope = query(h)
        along = (slope * head(qt, h).astype(f32)).astype(bf16)
        un = dot(feat, both[:E], (1, 0))
        un_dot = dot(along, both[:E], (1, 0)) + dot(feat, both[E:], (1, 0))
        inv = lax.rsqrt(jnp.mean(un * un, axis=-1, keepdims=True) + 1e-06)
        unnorm[h] = un
        scale[h] = inv
        normed[:, h * E : (h + 1) * E] = head(gain_ref, h) * norm_back(un, inv, un_dot)

    velocity = dot(normed[...].astype(bf16), weight[...], (1, 0))
    residual = (velocity - teach[...].astype(f32)).astype(bf16)
    res_ref[...] = residual
    ngrad[...] = dot(residual, weight[...], (1, 1))
    for h in range(H):
        weighted = head(gain_ref, h) * head(ngrad, h)
        grad = norm_back(unnorm[h], scale[h], weighted).astype(bf16)
        ugrad[h] = grad
        wide2[:, h * E : (h + 1) * E] = dot(query(h)[0], grad, (0, 0))

    def query_grads():
        for h in range(H):
            back = dot(ugrad[h], state(h), (1, 1))
            gq_ref[:, h * E : (h + 1) * E] = (query(h)[1] * back).astype(bf16)

    all_total(
        at, pieces[1], wide2, near2, sent2, out2, half2, mine2, parts2, sems[8:], query_grads
    )

    for h in range(H):
        total = head(wide2, h).astype(bf16)
        feat, slope = key_parts(h)
        cols = slice(h * E, (h + 1) * E)
        gk_ref[:, cols] = (slope * dot(head(v, h), total, (1, 1))).astype(bf16)
        gv_ref[:, cols] = dot(feat.astype(bf16), total, (1, 0)).astype(bf16)


def local(
    query_rows,
    key_rows,
    value_rows,
    query_tangent,
    key_tangent,
    value_tangent,
    teacher,
    out_weight,
    norm_gain,
    clip_length,
    block_mask,
):
    tok, width = query_rows.shape
    depth = lax.axis_size("sub")
    chips = lax.axis_size("seq") // 2 * depth
    padded = -(-width // LANES) * LANES
    vmem = pltpu.VMEM
    dma = pltpu.SemaphoreType.DMA
    pieces = []
    totals = []
    for size in (2 * E, E):
        piece = -(-(size * padded // LANES) // (32 * chips)) * 16
        pieces.append(piece)
        half = (chips * piece, LANES)
        full = (2 * chips * piece, LANES)
        totals += [vmem((size, padded), f32), vmem(full, f32), vmem(full, bf16), vmem(full, bf16)]
        totals += [vmem(half, bf16)] * 3
    arrays = (query_rows, key_rows, value_rows, query_tangent, key_tangent, value_tangent)
    arrays += (teacher, out_weight)
    anywhere = pl.BlockSpec(memory_space=pl.ANY)
    in_vmem = pl.BlockSpec(memory_space=vmem)
    in_smem = pl.BlockSpec(memory_space=pltpu.SMEM)
    return pl.pallas_call(
        functools.partial(step_kernel, chips, depth, pieces),
        out_shape=(
            jax.ShapeDtypeStruct(teacher.shape, bf16),
            jax.ShapeDtypeStruct(query_rows.shape, bf16),
            jax.ShapeDtypeStruct(query_rows.shape, bf16),
            jax.ShapeDtypeStruct(query_rows.shape, bf16),
        ),
        in_specs=[anywhere] * 8 + [in_vmem, in_smem, in_smem],
        out_specs=[in_vmem] * 4,
        scratch_shapes=[vmem(array.shape, array.dtype) for array in arrays]
        + [dma((8,))]
        + totals
        + [
            vmem((H, tok, E), f32),
            vmem((H, tok, 1), f32),
            vmem((tok, width), f32),
            vmem((tok, width), f32),
            vmem((H, tok, E), bf16),
        ]
        + ([dma, dma] + [dma((chips,))] * 6) * 2,
        compiler_params=pltpu.CompilerParams(collective_id=0, has_side_effects=True),
    )(*arrays, norm_gain[None, :], clip_length, block_mask)


def solution(mesh):
    return jax.shard_map(
        local,
        mesh=mesh,
        in_specs=(
            P(("seq", "sub"), None),
            P(("seq", "sub"), None),
            P(("seq", "sub"), None),
            P(("seq", "sub"), None),
            P(("seq", "sub"), None),
            P(("seq", "sub"), None),
            P(("seq", "sub"), None),
            P(),
            P(),
            P(),
            P(("seq", "sub")),
        ),
        out_specs=(
            P(("seq", "sub"), None),
            P(("seq", "sub"), None),
            P(("seq", "sub"), None),
            P(("seq", "sub"), None),
        ),
        check_vma=False,
    )
```

```python
import functools

import jax
import jax.numpy as jnp
from jax import lax
from jax.experimental import pallas as pl
from jax.experimental.pallas import tpu as pltpu
from jax.sharding import PartitionSpec as P

H = 10
E = 112
BLK = 64


MESH = pl.DeviceIdType.MESH
LANES = 128
f32 = jnp.float32
bf16 = jnp.bfloat16


def norm_back(unnorm, scale_inv, weighted):
    inner_mean = jnp.mean(unnorm * weighted, axis=0, keepdims=True)
    return scale_inv * weighted - unnorm * (scale_inv * scale_inv * scale_inv) * inner_mean


def dot(left, right, over):
    return lax.dot_general(left, right, ((over[:1], over[1:]), ((), ())), preferred_element_type=f32)


class Where:
    def __init__(self, chips, depth):
        seq = lax.axis_index("seq")
        self.sub = lax.axis_index("sub")
        self.depth = depth
        self.chips = chips
        self.core = lax.rem(seq, 2)
        self.chip = (seq // 2) * depth + self.sub
        self.partner = (seq + 1 - 2 * self.core, self.sub)

    def peer(self, index):
        return (index // self.depth) * 2 + self.core, lax.rem(index, self.depth)

    def ahead(self, step):
        return lax.rem(self.chip + step, self.chips)

    def behind(self, step):
        return lax.rem(self.chip + self.chips - step, self.chips)


def greet(at):
    barrier = pltpu.get_barrier_semaphore()
    pl.semaphore_signal(barrier, inc=1, device_id=at.partner, device_id_type=MESH)

    @pl.loop(1, at.chips)
    def _(step):
        pl.semaphore_signal(
            barrier, inc=1, device_id=at.peer(at.ahead(step)), device_id_type=MESH
        )


def all_total(at, piece, wide, near, sent, out, half, mine, parts, sems, between=None, after=None):
    s0, r0, s1, r1, s2, r2, s3, r3 = sems
    core, chip, chips = at.core, at.chip, at.chips

    def copy(src, dst, send, recv, to):
        return pltpu.make_async_remote_copy(
            src_ref=src,
            dst_ref=dst,
            send_sem=send,
            recv_sem=recv,
            device_id=to,
            device_id_type=MESH,
        )

    def rows(index, side=None):
        base = index if side is None else side * chips + index
        return pl.ds(pl.multiple_of(base * piece, 16), piece)

    def scatter(index, slot):
        return copy(
            mine.at[rows(index)], parts.at[rows(slot)], s1.at[index], r1.at[slot], at.peer(index)
        )

    def gather(index, slot):
        return copy(
            out.at[rows(chip, core)],
            out.at[rows(slot, core)],
            s2.at[index],
            r2.at[slot],
            at.peer(index),
        )

    def forward(index, side):
        return copy(
            out.at[rows(index, core)],
            out.at[rows(index, side)],
            s3.at[index],
            r3.at[index],
            at.partner,
        )

    size = wide.shape[0]
    for block in range(wide.shape[1] // LANES):
        lanes = wide[:, block * LANES : (block + 1) * LANES]
        near[block * size : (block + 1) * size, :] = lanes
        sent[block * size : (block + 1) * size, :] = lanes.astype(bf16)
    used = size * (wide.shape[1] // LANES)
    if used < near.shape[0]:
        near[used:, :] = jnp.zeros((near.shape[0] - used, LANES), f32)
        sent[used:, :] = jnp.zeros((near.shape[0] - used, LANES), bf16)

    other = pl.ds(pl.multiple_of((1 - core) * (chips * piece), 16), chips * piece)
    swap = copy(sent.at[other], half, s0, r0, at.partner)
    swap.start()
    if between is not None:
        between()
    swap.wait()

    def pair(index):
        return near[rows(index, core), :] + half[rows(index), :].astype(f32)

    @pl.loop(1, chips)
    def _(step):
        index = at.ahead(step)
        mine[rows(index), :] = pair(index).astype(bf16)
        scatter(index, chip).start()

    if after is not None:
        after()

    def add(step, acc):
        index = at.behind(step)
        scatter(index, index).wait_recv()
        return acc + parts[rows(index), :].astype(f32)

    out[rows(chip, core), :] = lax.fori_loop(1, chips, add, pair(chip)).astype(bf16)

    @pl.loop(1, chips)
    def _(step):
        gather(at.ahead(step), chip).start()

    forward(chip, core).start()

    @pl.loop(1, chips)
    def _(step):
        index = at.behind(step)
        gather(index, index).wait_recv()
        forward(index, core).start()

    @pl.loop(1, chips)
    def _(step):
        index = at.ahead(step)
        scatter(index, chip).wait_send()
        gather(index, chip).wait_send()

    @pl.loop(0, chips)
    def _(step):
        index = at.behind(step)
        forward(index, 1 - core).wait_recv()
        forward(index, core).wait_send()

    for block in range(wide.shape[1] // LANES):
        wide[:, block * LANES : (block + 1) * LANES] = out[
            block * size : (block + 1) * size, :
        ].astype(f32)


def step_kernel(
    chips, depth, pieces,
    q_hbm, k_hbm, v_hbm, qt_hbm, kt_hbm, vt_hbm, t_hbm, w_hbm, gain_ref, clip_ref, flags_ref,
    res_ref, gq_ref, gk_ref, gv_ref,
    q, k, v, qt, kt, vt, teach, weight, loads,
    wide1, near1, sent1, out1, half1, mine1, parts1,
    wide2, near2, sent2, out2, half2, mine2, parts2,
    unnorm, scale, normed, ngrad, ugrad, turned, gain,
    *sems,
):
    at = Where(chips, depth)
    tok = q.shape[1]
    incoming = [
        pltpu.make_async_copy(src, dst, loads.at[i])
        for i, (src, dst) in enumerate(
            [
                (k_hbm, k),
                (v_hbm, v),
                (kt_hbm, kt),
                (vt_hbm, vt),
                (w_hbm, weight),
                (q_hbm, q),
                (qt_hbm, qt),
                (t_hbm, teach),
            ]
        )
    ]
    greet(at)
    for load in incoming:
        load.start()

    token = lax.broadcasted_iota(jnp.int32, (8, tok), 1)
    device = lax.axis_index("seq") * depth + at.sub
    kept = jnp.zeros((8, tok), jnp.int32)
    for block in range(tok // BLK):
        inside = (token >= block * BLK) & (token < (block + 1) * BLK)
        kept = jnp.where(inside, flags_ref[block], kept)
    before = token + device * tok < clip_ref[0]
    valid = jnp.where(before & (kept == 1), 1.0, 0.0).astype(f32)[:1]

    def head(ref, h):
        return ref[h * E : (h + 1) * E, :]

    def square(ref, h):
        return ref[:, h * E : (h + 1) * E].astype(bf16)

    def key_parts(h):
        keys = head(k, h).astype(f32)
        slope = jnp.where(keys > 0, 1.0, 0.0) * valid
        return jnp.maximum(keys, 0.0) * valid, slope

    edge = wide1.shape[1] - LANES
    wide1[:, edge:] = jnp.zeros((wide1.shape[0], LANES), f32)
    wide2[:, edge:] = jnp.zeros((wide2.shape[0], LANES), f32)
    for load in incoming[:4]:
        load.wait()
    for h in range(H):
        feat, slope = key_parts(h)
        feat = feat.astype(bf16)
        along = (slope * head(kt, h).astype(f32)).astype(bf16)
        vals = head(v, h)
        cols = slice(h * E, (h + 1) * E)
        wide1[:E, cols] = dot(vals, feat, (1, 1))
        wide1[E:, cols] = dot(vals, along, (1, 1)) + dot(head(vt, h), feat, (1, 1))

    def prepare():
        row = lax.broadcasted_iota(jnp.int32, (E, E), 0)
        col = lax.broadcasted_iota(jnp.int32, (E, E), 1)
        for h in range(H):
            spread = jnp.where(row == col, gain_ref[:, h * E : (h + 1) * E], 0.0)
            gain[h * E : (h + 1) * E, :] = jnp.sum(spread, axis=1, keepdims=True)
        for load in incoming[4:]:
            load.wait()
        for start in range(0, weight.shape[1], 256):
            stop = min(start + 256, weight.shape[1])
            turned[start:stop, :] = weight[:, start:stop].T

    pl.semaphore_wait(pltpu.get_barrier_semaphore(), chips)
    all_total(
        at, pieces[0], wide1, near1, sent1, out1, half1, mine1, parts1, sems[:8], None, prepare
    )

    def query(h):
        rows = head(q, h).astype(f32)
        return jnp.maximum(rows, 0.0).astype(bf16), jnp.where(rows > 0, 1.0, 0.0).astype(f32)

    for h in range(H):
        rows = slice(h * E, (h + 1) * E)
        both = square(wide1, h)
        feat, slope = query(h)
        along = (slope * head(qt, h).astype(f32)).astype(bf16)
        un = dot(both[:E], feat, (1, 0))
        un_dot = dot(both[:E], along, (1, 0)) + dot(both[E:], feat, (1, 0))
        inv = lax.rsqrt(jnp.mean(un * un, axis=0, keepdims=True) + 1e-06)
        unnorm[rows, :] = un
        scale[h] = inv
        normed[rows, :] = (gain[rows, :] * norm_back(un, inv, un_dot)).astype(bf16)

    velocity = dot(turned[...], normed[...], (1, 0))
    res_ref[...] = (velocity - teach[...].astype(f32)).astype(bf16)
    ngrad[...] = dot(weight[...], res_ref[...], (1, 0))
    for h in range(H):
        rows = slice(h * E, (h + 1) * E)
        weighted = gain[rows, :] * head(ngrad, h)
        grad = norm_back(head(unnorm, h), scale[h], weighted).astype(bf16)
        ugrad[rows, :] = grad
        wide2[:, h * E : (h + 1) * E] = dot(grad, query(h)[0], (1, 1))

    def query_grads():
        for h in range(H):
            back = dot(square(wide1, h)[:E], head(ugrad, h), (0, 0))
            gq_ref[h * E : (h + 1) * E, :] = (query(h)[1] * back).astype(bf16)

    all_total(
        at, pieces[1], wide2, near2, sent2, out2, half2, mine2, parts2, sems[8:], None, query_grads
    )

    for h in range(H):
        total = square(wide2, h)
        feat, slope = key_parts(h)
        rows = slice(h * E, (h + 1) * E)
        gk_ref[rows, :] = (slope * dot(total, head(v, h), (0, 0))).astype(bf16)
        gv_ref[rows, :] = dot(total, feat.astype(bf16), (1, 0)).astype(bf16)


def local(
    query_rows,
    key_rows,
    value_rows,
    query_tangent,
    key_tangent,
    value_tangent,
    teacher,
    out_weight,
    norm_gain,
    clip_length,
    block_mask,
):
    tok, width = query_rows.shape
    depth = lax.axis_size("sub")
    chips = lax.axis_size("seq") // 2 * depth
    padded = -(-width // LANES) * LANES
    vmem = pltpu.VMEM
    dma = pltpu.SemaphoreType.DMA
    pieces = []
    totals = []
    for size in (2 * E, E):
        piece = -(-(size * padded // LANES) // (32 * chips)) * 16
        pieces.append(piece)
        half = (chips * piece, LANES)
        full = (2 * chips * piece, LANES)
        totals += [vmem((size, padded), f32), vmem(full, f32), vmem(full, bf16), vmem(full, bf16)]
        totals += [vmem(half, bf16)] * 3
    arrays = (query_rows, key_rows, value_rows, query_tangent, key_tangent, value_tangent)
    arrays = tuple(array.T for array in arrays + (teacher,)) + (out_weight,)
    anywhere = pl.BlockSpec(memory_space=pl.ANY)
    in_vmem = pl.BlockSpec(memory_space=vmem)
    in_smem = pl.BlockSpec(memory_space=pltpu.SMEM)
    outs = pl.pallas_call(
        functools.partial(step_kernel, chips, depth, pieces),
        out_shape=(
            jax.ShapeDtypeStruct(teacher.shape[::-1], bf16),
            jax.ShapeDtypeStruct((width, tok), bf16),
            jax.ShapeDtypeStruct((width, tok), bf16),
            jax.ShapeDtypeStruct((width, tok), bf16),
        ),
        in_specs=[anywhere] * 8 + [in_vmem, in_smem, in_smem],
        out_specs=[in_vmem] * 4,
        scratch_shapes=[vmem(array.shape, array.dtype) for array in arrays]
        + [dma((8,))]
        + totals
        + [
            vmem((width, tok), f32),
            vmem((H, 1, tok), f32),
            vmem((width, tok), bf16),
            vmem((width, tok), f32),
            vmem((width, tok), bf16),
            vmem(out_weight.shape[::-1], bf16),
            vmem((width, 1), f32),
        ]
        + ([dma, dma] + [dma((chips,))] * 6) * 2,
        compiler_params=pltpu.CompilerParams(collective_id=0, has_side_effects=True),
    )(*arrays, norm_gain[None, :], clip_length, block_mask)
    return tuple(out.T for out in outs)


def solution(mesh):
    return jax.shard_map(
        local,
        mesh=mesh,
        in_specs=(
            P(("seq", "sub"), None),
            P(("seq", "sub"), None),
            P(("seq", "sub"), None),
            P(("seq", "sub"), None),
            P(("seq", "sub"), None),
            P(("seq", "sub"), None),
            P(("seq", "sub"), None),
            P(),
            P(),
            P(),
            P(("seq", "sub")),
        ),
        out_specs=(
            P(("seq", "sub"), None),
            P(("seq", "sub"), None),
            P(("seq", "sub"), None),
            P(("seq", "sub"), None),
        ),
        check_vma=False,
    )
```

```python
import functools

import jax
import jax.numpy as jnp
from jax import lax
from jax.experimental import pallas as pl
from jax.experimental.pallas import tpu as pltpu
from jax.sharding import PartitionSpec as P

H = 10
E = 112
BLK = 64


MESH = pl.DeviceIdType.MESH
LANES = 128
f32 = jnp.float32
bf16 = jnp.bfloat16


def norm_back(unnorm, scale_inv, weighted):
    inner_mean = jnp.mean(unnorm * weighted, axis=0, keepdims=True)
    return scale_inv * weighted - unnorm * (scale_inv * scale_inv * scale_inv) * inner_mean


def dot(left, right, over):
    return lax.dot_general(left, right, ((over[:1], over[1:]), ((), ())), preferred_element_type=f32)


class Where:
    def __init__(self, chips, depth):
        seq = lax.axis_index("seq")
        self.sub = lax.axis_index("sub")
        self.depth = depth
        self.chips = chips
        self.core = lax.rem(seq, 2)
        self.chip = (seq // 2) * depth + self.sub
        self.partner = (seq + 1 - 2 * self.core, self.sub)

    def peer(self, index):
        return (index // self.depth) * 2 + self.core, lax.rem(index, self.depth)

    def ahead(self, step):
        return lax.rem(self.chip + step, self.chips)

    def behind(self, step):
        return lax.rem(self.chip + self.chips - step, self.chips)


def greet(at):
    barrier = pltpu.get_barrier_semaphore()
    pl.semaphore_signal(barrier, inc=1, device_id=at.partner, device_id_type=MESH)

    @pl.loop(1, at.chips)
    def _(step):
        pl.semaphore_signal(
            barrier, inc=1, device_id=at.peer(at.ahead(step)), device_id_type=MESH
        )


def all_total(at, piece, wide, near, sent, out, half, mine, parts, sems, between=None, after=None):
    s0, r0, s1, r1, s2, r2, s3, r3 = sems
    core, chip, chips = at.core, at.chip, at.chips

    def copy(src, dst, send, recv, to):
        return pltpu.make_async_remote_copy(
            src_ref=src,
            dst_ref=dst,
            send_sem=send,
            recv_sem=recv,
            device_id=to,
            device_id_type=MESH,
        )

    def rows(index, side=None):
        base = index if side is None else side * chips + index
        return pl.ds(pl.multiple_of(base * piece, 16), piece)

    def scatter(index, slot):
        return copy(
            mine.at[rows(index)], parts.at[rows(slot)], s1.at[index], r1.at[slot], at.peer(index)
        )

    def gather(index, slot):
        return copy(
            out.at[rows(chip, core)],
            out.at[rows(slot, core)],
            s2.at[index],
            r2.at[slot],
            at.peer(index),
        )

    def forward(index, side):
        return copy(
            out.at[rows(index, core)],
            out.at[rows(index, side)],
            s3.at[index],
            r3.at[index],
            at.partner,
        )

    size = wide.shape[0]
    for block in range(wide.shape[1] // LANES):
        lanes = wide[:, block * LANES : (block + 1) * LANES]
        near[block * size : (block + 1) * size, :] = lanes
        sent[block * size : (block + 1) * size, :] = lanes.astype(bf16)
    used = size * (wide.shape[1] // LANES)
    if used < near.shape[0]:
        near[used:, :] = jnp.zeros((near.shape[0] - used, LANES), f32)
        sent[used:, :] = jnp.zeros((near.shape[0] - used, LANES), bf16)

    other = pl.ds(pl.multiple_of((1 - core) * (chips * piece), 16), chips * piece)
    swap = copy(sent.at[other], half, s0, r0, at.partner)
    swap.start()
    if between is not None:
        between()
    swap.wait()

    def pair(index):
        return near[rows(index, core), :] + half[rows(index), :].astype(f32)

    @pl.loop(1, chips)
    def _(step):
        index = at.ahead(step)
        mine[rows(index), :] = pair(index).astype(bf16)
        scatter(index, chip).start()

    if after is not None:
        after()

    def add(step, acc):
        index = at.behind(step)
        scatter(index, index).wait_recv()
        return acc + parts[rows(index), :].astype(f32)

    out[rows(chip, core), :] = lax.fori_loop(1, chips, add, pair(chip)).astype(bf16)

    @pl.loop(1, chips)
    def _(step):
        gather(at.ahead(step), chip).start()

    forward(chip, core).start()

    @pl.loop(1, chips)
    def _(step):
        index = at.behind(step)
        gather(index, index).wait_recv()
        forward(index, core).start()

    @pl.loop(1, chips)
    def _(step):
        index = at.ahead(step)
        scatter(index, chip).wait_send()
        gather(index, chip).wait_send()

    @pl.loop(0, chips)
    def _(step):
        index = at.behind(step)
        forward(index, 1 - core).wait_recv()
        forward(index, core).wait_send()

    for block in range(wide.shape[1] // LANES):
        wide[:, block * LANES : (block + 1) * LANES] = out[
            block * size : (block + 1) * size, :
        ].astype(f32)


def kept_tokens(tok, first, clip_ref, flags_ref):
    token = lax.broadcasted_iota(jnp.int32, (8, tok), 1)
    kept = jnp.zeros((8, tok), jnp.int32)
    for block in range(tok // BLK):
        inside = (token >= block * BLK) & (token < (block + 1) * BLK)
        kept = jnp.where(inside, flags_ref[block], kept)
    before = token + first < clip_ref[0]
    return jnp.where(before & (kept == 1), 1.0, 0.0).astype(f32)[:1]


def step_kernel(
    chips, depth, pieces,
    q_hbm, k_hbm, v_hbm, qt_hbm, kt_hbm, vt_hbm, t_hbm, w_hbm, gain_ref, clip_ref, flags_ref,
    res_hbm, gq_hbm, grad_ref,
    q, k, v, qt, kt, vt, teach, weight, loads,
    wide1, near1, sent1, out1, half1, mine1, parts1,
    wide2, near2, sent2, out2, half2, mine2, parts2,
    unnorm, scale, normed, ngrad, ugrad, turned, gain, res_ref, gq_ref, stores,
    *sems,
):
    at = Where(chips, depth)
    tok = q.shape[1]
    incoming = [
        pltpu.make_async_copy(src, dst, loads.at[i])
        for i, (src, dst) in enumerate(
            [
                (k_hbm, k),
                (v_hbm, v),
                (kt_hbm, kt),
                (vt_hbm, vt),
                (w_hbm, weight),
                (q_hbm, q),
                (qt_hbm, qt),
                (t_hbm, teach),
            ]
        )
    ]
    greet(at)
    for load in incoming:
        load.start()

    device = lax.axis_index("seq") * depth + at.sub
    valid = kept_tokens(tok, device * tok, clip_ref, flags_ref)

    def head(ref, h):
        return ref[h * E : (h + 1) * E, :]

    def square(ref, h):
        return ref[:, h * E : (h + 1) * E].astype(bf16)

    def key_parts(h):
        keys = head(k, h).astype(f32)
        slope = jnp.where(keys > 0, 1.0, 0.0) * valid
        return jnp.maximum(keys, 0.0) * valid, slope

    edge = wide1.shape[1] - LANES
    wide1[:, edge:] = jnp.zeros((wide1.shape[0], LANES), f32)
    wide2[:, edge:] = jnp.zeros((wide2.shape[0], LANES), f32)
    for load in incoming[:4]:
        load.wait()
    for h in range(H):
        feat, slope = key_parts(h)
        feat = feat.astype(bf16)
        along = (slope * head(kt, h).astype(f32)).astype(bf16)
        vals = head(v, h)
        cols = slice(h * E, (h + 1) * E)
        wide1[:E, cols] = dot(vals, feat, (1, 1))
        wide1[E:, cols] = dot(vals, along, (1, 1)) + dot(head(vt, h), feat, (1, 1))

    def prepare():
        row = lax.broadcasted_iota(jnp.int32, (E, E), 0)
        col = lax.broadcasted_iota(jnp.int32, (E, E), 1)
        for h in range(H):
            spread = jnp.where(row == col, gain_ref[:, h * E : (h + 1) * E], 0.0)
            gain[h * E : (h + 1) * E, :] = jnp.sum(spread, axis=1, keepdims=True)
        for load in incoming[4:]:
            load.wait()
        for start in range(0, weight.shape[1], 256):
            stop = min(start + 256, weight.shape[1])
            turned[start:stop, :] = weight[:, start:stop].T

    pl.semaphore_wait(pltpu.get_barrier_semaphore(), chips)
    all_total(
        at, pieces[0], wide1, near1, sent1, out1, half1, mine1, parts1, sems[:8], None, prepare
    )

    def query(h):
        rows = head(q, h).astype(f32)
        return jnp.maximum(rows, 0.0).astype(bf16), jnp.where(rows > 0, 1.0, 0.0).astype(f32)

    for h in range(H):
        rows = slice(h * E, (h + 1) * E)
        both = square(wide1, h)
        feat, slope = query(h)
        along = (slope * head(qt, h).astype(f32)).astype(bf16)
        un = dot(both[:E], feat, (1, 0))
        un_dot = dot(both[:E], along, (1, 0)) + dot(both[E:], feat, (1, 0))
        inv = lax.rsqrt(jnp.mean(un * un, axis=0, keepdims=True) + 1e-06)
        unnorm[rows, :] = un
        scale[h] = inv
        normed[rows, :] = (gain[rows, :] * norm_back(un, inv, un_dot)).astype(bf16)

    velocity = dot(turned[...], normed[...], (1, 0))
    res_ref[...] = (velocity - teach[...].astype(f32)).astype(bf16)
    res_out = pltpu.make_async_copy(res_ref, res_hbm, stores.at[0])
    gq_out = pltpu.make_async_copy(gq_ref, gq_hbm, stores.at[1])
    res_out.start()
    ngrad[...] = dot(weight[...], res_ref[...], (1, 0))
    for h in range(H):
        rows = slice(h * E, (h + 1) * E)
        weighted = gain[rows, :] * head(ngrad, h)
        grad = norm_back(head(unnorm, h), scale[h], weighted).astype(bf16)
        ugrad[rows, :] = grad
        wide2[:, h * E : (h + 1) * E] = dot(grad, query(h)[0], (1, 1))

    def query_grads():
        for h in range(H):
            back = dot(square(wide1, h)[:E], head(ugrad, h), (0, 0))
            gq_ref[h * E : (h + 1) * E, :] = (query(h)[1] * back).astype(bf16)
        gq_out.start()

    all_total(
        at, pieces[1], wide2, near2, sent2, out2, half2, mine2, parts2, sems[8:], None, query_grads
    )

    grad_ref[...] = wide2[...].astype(bf16)
    res_out.wait()
    gq_out.wait()


def finish_kernel(
    first_ref, k_hbm, v_hbm, res_hbm, gq_hbm, grad_ref, clip_ref, flags_ref,
    res_out, gq_out, gk_out, gv_out,
    k, v, res, gq, gk, gv, loads, stores,
):
    tok = k.shape[1]
    pairs = [(k_hbm, k), (v_hbm, v), (res_hbm, res), (gq_hbm, gq)]
    incoming = [pltpu.make_async_copy(*pair, loads.at[i]) for i, pair in enumerate(pairs)]
    pairs = [(res, res_out), (gq, gq_out), (gk, gk_out), (gv, gv_out)]
    outgoing = [pltpu.make_async_copy(*pair, stores.at[i]) for i, pair in enumerate(pairs)]
    for load in incoming:
        load.start()
    valid = kept_tokens(tok, first_ref[0], clip_ref, flags_ref)
    incoming[0].wait()
    incoming[1].wait()
    for h in range(H):
        rows = slice(h * E, (h + 1) * E)
        total = grad_ref[:, rows]
        keys = k[rows, :].astype(f32)
        slope = jnp.where(keys > 0, 1.0, 0.0) * valid
        feat = (jnp.maximum(keys, 0.0) * valid).astype(bf16)
        gk[rows, :] = (slope * dot(total, v[rows, :], (0, 0))).astype(bf16)
        gv[rows, :] = dot(total, feat, (1, 0)).astype(bf16)
        if h == 1:
            for load, store in zip(incoming[2:], outgoing[:2]):
                load.wait()
                store.start()
    outgoing[2].start()
    outgoing[3].start()
    for store in outgoing:
        store.wait()


def local(
    query_rows,
    key_rows,
    value_rows,
    query_tangent,
    key_tangent,
    value_tangent,
    teacher,
    out_weight,
    norm_gain,
    clip_length,
    block_mask,
):
    tok, width = query_rows.shape
    depth = lax.axis_size("sub")
    chips = lax.axis_size("seq") // 2 * depth
    padded = -(-width // LANES) * LANES
    vmem = pltpu.VMEM
    dma = pltpu.SemaphoreType.DMA
    pieces = []
    totals = []
    for size in (2 * E, E):
        piece = -(-(size * padded // LANES) // (32 * chips)) * 16
        pieces.append(piece)
        half = (chips * piece, LANES)
        full = (2 * chips * piece, LANES)
        totals += [vmem((size, padded), f32), vmem(full, f32), vmem(full, bf16), vmem(full, bf16)]
        totals += [vmem(half, bf16)] * 3
    arrays = (query_rows, key_rows, value_rows, query_tangent, key_tangent, value_tangent)
    arrays = tuple(array.T for array in arrays + (teacher,)) + (out_weight,)
    anywhere = pl.BlockSpec(memory_space=pl.ANY)
    in_vmem = pl.BlockSpec(memory_space=vmem)
    in_smem = pl.BlockSpec(memory_space=pltpu.SMEM)
    wide_t = jax.ShapeDtypeStruct((width, tok), bf16)
    res_t = jax.ShapeDtypeStruct(teacher.shape[::-1], bf16)
    res, grad_query, grad = pl.pallas_call(
        functools.partial(step_kernel, chips, depth, pieces),
        out_shape=(res_t, wide_t, jax.ShapeDtypeStruct((E, padded), bf16)),
        in_specs=[anywhere] * 8 + [in_vmem, in_smem, in_smem],
        out_specs=[anywhere, anywhere, in_vmem],
        scratch_shapes=[vmem(array.shape, array.dtype) for array in arrays]
        + [dma((8,))]
        + totals
        + [
            vmem((width, tok), f32),
            vmem((H, 1, tok), f32),
            vmem((width, tok), bf16),
            vmem((width, tok), f32),
            vmem((width, tok), bf16),
            vmem(out_weight.shape[::-1], bf16),
            vmem((width, 1), f32),
            vmem(res_t.shape, bf16),
            vmem((width, tok), bf16),
            dma((2,)),
        ]
        + ([dma, dma] + [dma((chips,))] * 6) * 2,
        compiler_params=pltpu.CompilerParams(collective_id=0, has_side_effects=True),
    )(*arrays, norm_gain[None, :], clip_length, block_mask)
    first = (lax.axis_index("seq") * depth + lax.axis_index("sub")) * tok
    outs = pl.pallas_call(
        finish_kernel,
        out_shape=(res_t, wide_t, wide_t, wide_t),
        in_specs=[in_smem] + [anywhere] * 4 + [in_vmem, in_smem, in_smem],
        out_specs=[anywhere] * 4,
        scratch_shapes=[vmem(wide_t.shape, bf16)] * 2
        + [vmem(res_t.shape, bf16)]
        + [vmem(wide_t.shape, bf16)] * 3
        + [dma((4,)), dma((4,))],
    )(first[None], arrays[1], arrays[2], res, grad_query, grad, clip_length, block_mask)
    return tuple(out.T for out in outs)


def solution(mesh):
    return jax.shard_map(
        local,
        mesh=mesh,
        in_specs=(
            P(("seq", "sub"), None),
            P(("seq", "sub"), None),
            P(("seq", "sub"), None),
            P(("seq", "sub"), None),
            P(("seq", "sub"), None),
            P(("seq", "sub"), None),
            P(("seq", "sub"), None),
            P(),
            P(),
            P(),
            P(("seq", "sub")),
        ),
        out_specs=(
            P(("seq", "sub"), None),
            P(("seq", "sub"), None),
            P(("seq", "sub"), None),
            P(("seq", "sub"), None),
        ),
        check_vma=False,
    )
```

```python
import functools

import jax
import jax.numpy as jnp
from jax import lax
from jax.experimental import pallas as pl
from jax.experimental.pallas import tpu as pltpu
from jax.sharding import PartitionSpec as P

H = 10
E = 112
BLK = 64


MESH = pl.DeviceIdType.MESH
LANES = 128
f32 = jnp.float32
bf16 = jnp.bfloat16


def norm_back(unnorm, scale_inv, weighted):
    inner_mean = jnp.mean(unnorm * weighted, axis=0, keepdims=True)
    return scale_inv * weighted - unnorm * (scale_inv * scale_inv * scale_inv) * inner_mean


def dot(left, right, over):
    return lax.dot_general(left, right, ((over[:1], over[1:]), ((), ())), preferred_element_type=f32)


class Where:
    def __init__(self, chips, depth):
        seq = lax.axis_index("seq")
        self.sub = lax.axis_index("sub")
        self.depth = depth
        self.chips = chips
        self.core = lax.rem(seq, 2)
        self.plane = seq // 2
        self.planes = chips // depth
        self.chip = self.plane * depth + self.sub
        self.partner = (seq + 1 - 2 * self.core, self.sub)

    def peer(self, index):
        return (index // self.depth) * 2 + self.core, lax.rem(index, self.depth)

    def ahead(self, step):
        return lax.rem(self.chip + step, self.chips)

    def behind(self, step):
        return lax.rem(self.chip + self.chips - step, self.chips)


def greet(at):
    barrier = pltpu.get_barrier_semaphore()
    pl.semaphore_signal(barrier, inc=1, device_id=at.partner, device_id_type=MESH)

    @pl.loop(1, at.planes)
    def _(step):
        to = at.peer(lax.rem(at.plane + step, at.planes) * at.depth + at.sub)
        pl.semaphore_signal(barrier, inc=1, device_id=to, device_id_type=MESH)

    @pl.loop(1, at.depth)
    def _(step):
        to = at.peer(at.plane * at.depth + lax.rem(at.sub + step, at.depth))
        pl.semaphore_signal(barrier, inc=1, device_id=to, device_id_type=MESH)


def all_total(at, piece, wide, near, sent, out, half, mine, parts, sems, hooks):
    s0, r0, s1, r1, s2, r2, s3, r3, s4, r4, s5, r5 = sems
    plane, planes, sub, depth = at.plane, at.planes, at.sub, at.depth
    core, chip, chips = at.core, at.chip, at.chips

    def copy(src, dst, send, recv, to):
        return pltpu.make_async_remote_copy(
            src_ref=src,
            dst_ref=dst,
            send_sem=send,
            recv_sem=recv,
            device_id=to,
            device_id_type=MESH,
        )

    def rows(index, side=None):
        base = index if side is None else side * chips + index
        return pl.ds(pl.multiple_of(base * piece, 16), piece)

    def spot(side, level):
        return side * depth + level

    def plane_scatter(side, level, slot):
        return copy(
            mine.at[rows(spot(side, level))],
            parts.at[rows(spot(slot, level))],
            s1.at[spot(side, level)],
            r1.at[spot(slot, level)],
            at.peer(spot(side, sub)),
        )

    def deep_scatter(level, slot):
        return copy(
            mine.at[rows(spot(plane, level))],
            parts.at[rows(spot(plane, slot))],
            s2.at[level],
            r2.at[slot],
            at.peer(spot(plane, level)),
        )

    def deep_gather(level, slot):
        return copy(
            out.at[rows(chip, core)],
            out.at[rows(spot(plane, slot), core)],
            s3.at[level],
            r3.at[slot],
            at.peer(spot(plane, level)),
        )

    def plane_gather(side, level, slot):
        return copy(
            out.at[rows(spot(plane, level), core)],
            out.at[rows(spot(slot, level), core)],
            s4.at[spot(side, level)],
            r4.at[spot(slot, level)],
            at.peer(spot(side, sub)),
        )

    def forward(index, side):
        return copy(
            out.at[rows(index, core)],
            out.at[rows(index, side)],
            s5.at[index],
            r5.at[index],
            at.partner,
        )

    def side_of(step):
        return lax.rem(plane + step, planes)

    def side_from(step):
        return lax.rem(plane + planes - step, planes)

    def level_of(step):
        return lax.rem(sub + step, depth)

    def level_from(step):
        return lax.rem(sub + depth - step, depth)

    size = wide.shape[0]
    for block in range(wide.shape[1] // LANES):
        lanes = wide[:, block * LANES : (block + 1) * LANES]
        near[block * size : (block + 1) * size, :] = lanes
        sent[block * size : (block + 1) * size, :] = lanes.astype(bf16)
    used = size * (wide.shape[1] // LANES)
    if used < near.shape[0]:
        near[used:, :] = jnp.zeros((near.shape[0] - used, LANES), f32)
        sent[used:, :] = jnp.zeros((near.shape[0] - used, LANES), bf16)

    other = pl.ds(pl.multiple_of((1 - core) * (chips * piece), 16), chips * piece)
    swap = copy(sent.at[other], half, s0, r0, at.partner)
    swap.start()
    swap.wait()

    def pair(index):
        return near[rows(index, core), :] + half[rows(index), :].astype(f32)

    @pl.loop(1, depth + 1)
    def _(step):
        level = level_of(step)

        @pl.loop(1, planes)
        def _(turn):
            side = side_of(turn)
            mine[rows(spot(side, level)), :] = pair(spot(side, level)).astype(bf16)
            plane_scatter(side, level, plane).start()

    hooks[0]()

    def plane_sum(level):
        def add(turn, acc):
            side = side_from(turn)
            plane_scatter(side, level, side).wait_recv()
            return acc + parts[rows(spot(side, level)), :].astype(f32)

        return lax.fori_loop(1, planes, add, pair(spot(plane, level)))

    @pl.loop(1, depth)
    def _(step):
        level = level_of(step)
        mine[rows(spot(plane, level)), :] = plane_sum(level).astype(bf16)
        deep_scatter(level, sub).start()

    own = plane_sum(sub)
    hooks[1]()

    def deep_add(step, acc):
        level = level_from(step)
        deep_scatter(level, level).wait_recv()
        return acc + parts[rows(spot(plane, level)), :].astype(f32)

    out[rows(chip, core), :] = lax.fori_loop(1, depth, deep_add, own).astype(bf16)

    @pl.loop(1, depth)
    def _(step):
        deep_gather(level_of(step), sub).start()

    def spread(level):
        @pl.loop(1, planes)
        def _(turn):
            plane_gather(side_of(turn), level, plane).start()

        forward(spot(plane, level), core).start()

    spread(sub)

    @pl.loop(1, depth)
    def _(step):
        level = level_from(step)
        deep_gather(level, level).wait_recv()
        spread(level)

    @pl.loop(0, depth)
    def _(step):
        level = level_from(step)

        @pl.loop(1, planes)
        def _(turn):
            side = side_from(turn)
            plane_gather(side, level, side).wait_recv()
            forward(spot(side, level), core).start()

    @pl.loop(1, depth)
    def _(step):
        deep_scatter(level_of(step), sub).wait_send()
        deep_gather(level_of(step), sub).wait_send()

    @pl.loop(0, depth)
    def _(step):
        level = level_from(step)

        @pl.loop(1, planes)
        def _(turn):
            plane_scatter(side_of(turn), level, plane).wait_send()
            plane_gather(side_of(turn), level, plane).wait_send()

    @pl.loop(0, chips)
    def _(step):
        index = at.behind(step)
        forward(index, 1 - core).wait_recv()
        forward(index, core).wait_send()

    for block in range(wide.shape[1] // LANES):
        wide[:, block * LANES : (block + 1) * LANES] = out[
            block * size : (block + 1) * size, :
        ].astype(f32)


def kept_tokens(tok, first, clip_ref, flags_ref):
    token = lax.broadcasted_iota(jnp.int32, (8, tok), 1)
    kept = jnp.zeros((8, tok), jnp.int32)
    for block in range(tok // BLK):
        inside = (token >= block * BLK) & (token < (block + 1) * BLK)
        kept = jnp.where(inside, flags_ref[block], kept)
    before = token + first < clip_ref[0]
    return jnp.where(before & (kept == 1), 1.0, 0.0).astype(f32)[:1]


def step_kernel(
    chips, depth, pieces,
    q_hbm, k_hbm, v_hbm, qt_hbm, kt_hbm, vt_hbm, t_hbm, w_hbm, gain_ref, clip_ref, flags_ref,
    res_hbm, gq_hbm, grad_ref,
    q, k, v, qt, kt, vt, teach, weight, loads,
    wide1, near1, sent1, out1, half1, mine1, parts1,
    wide2, near2, sent2, out2, half2, mine2, parts2,
    unnorm, scale, normed, ngrad, ugrad, turned, gain, res_ref, gq_ref, stores,
    *sems,
):
    at = Where(chips, depth)
    tok = q.shape[1]
    incoming = [
        pltpu.make_async_copy(src, dst, loads.at[i])
        for i, (src, dst) in enumerate(
            [
                (k_hbm, k),
                (v_hbm, v),
                (kt_hbm, kt),
                (vt_hbm, vt),
                (w_hbm, weight),
                (q_hbm, q),
                (qt_hbm, qt),
                (t_hbm, teach),
            ]
        )
    ]
    greet(at)
    for load in incoming:
        load.start()

    device = lax.axis_index("seq") * depth + at.sub
    valid = kept_tokens(tok, device * tok, clip_ref, flags_ref)

    def head(ref, h):
        return ref[h * E : (h + 1) * E, :]

    def square(ref, h):
        return ref[:, h * E : (h + 1) * E].astype(bf16)

    def key_parts(h):
        keys = head(k, h).astype(f32)
        slope = jnp.where(keys > 0, 1.0, 0.0) * valid
        return jnp.maximum(keys, 0.0) * valid, slope

    edge = wide1.shape[1] - LANES
    wide1[:, edge:] = jnp.zeros((wide1.shape[0], LANES), f32)
    wide2[:, edge:] = jnp.zeros((wide2.shape[0], LANES), f32)
    for load in incoming[:4]:
        load.wait()
    for h in range(H):
        feat, slope = key_parts(h)
        feat = feat.astype(bf16)
        along = (slope * head(kt, h).astype(f32)).astype(bf16)
        vals = head(v, h)
        cols = slice(h * E, (h + 1) * E)
        wide1[:E, cols] = dot(vals, feat, (1, 1))
        wide1[E:, cols] = dot(vals, along, (1, 1)) + dot(head(vt, h), feat, (1, 1))

    def prepare():
        row = lax.broadcasted_iota(jnp.int32, (E, E), 0)
        col = lax.broadcasted_iota(jnp.int32, (E, E), 1)
        for h in range(H):
            spread = jnp.where(row == col, gain_ref[:, h * E : (h + 1) * E], 0.0)
            gain[h * E : (h + 1) * E, :] = jnp.sum(spread, axis=1, keepdims=True)
        for load in incoming[4:]:
            load.wait()
        turn(0, 5)

    def turn(first, last):
        for block in range(first, last):
            start = block * 256
            stop = min(start + 256, weight.shape[1])
            turned[start:stop, :] = weight[:, start:stop].T

    def turn_rest():
        turn(5, pl.cdiv(weight.shape[1], 256))

    pl.semaphore_wait(pltpu.get_barrier_semaphore(), at.planes + depth - 1)
    all_total(
        at, pieces[0], wide1, near1, sent1, out1, half1, mine1, parts1, sems[:12], (prepare, turn_rest)
    )

    def query(h):
        rows = head(q, h).astype(f32)
        return jnp.maximum(rows, 0.0).astype(bf16), jnp.where(rows > 0, 1.0, 0.0).astype(f32)

    for h in range(H):
        rows = slice(h * E, (h + 1) * E)
        both = square(wide1, h)
        feat, slope = query(h)
        along = (slope * head(qt, h).astype(f32)).astype(bf16)
        un = dot(both[:E], feat, (1, 0))
        un_dot = dot(both[:E], along, (1, 0)) + dot(both[E:], feat, (1, 0))
        inv = lax.rsqrt(jnp.mean(un * un, axis=0, keepdims=True) + 1e-06)
        unnorm[rows, :] = un
        scale[h] = inv
        normed[rows, :] = (gain[rows, :] * norm_back(un, inv, un_dot)).astype(bf16)

    velocity = dot(turned[...], normed[...], (1, 0))
    res_ref[...] = (velocity - teach[...].astype(f32)).astype(bf16)
    res_out = pltpu.make_async_copy(res_ref, res_hbm, stores.at[0])
    gq_out = pltpu.make_async_copy(gq_ref, gq_hbm, stores.at[1])
    res_out.start()
    ngrad[...] = dot(weight[...], res_ref[...], (1, 0))
    for h in range(H):
        rows = slice(h * E, (h + 1) * E)
        weighted = gain[rows, :] * head(ngrad, h)
        grad = norm_back(head(unnorm, h), scale[h], weighted).astype(bf16)
        ugrad[rows, :] = grad
        wide2[:, h * E : (h + 1) * E] = dot(grad, query(h)[0], (1, 1))

    def query_grads():
        for h in range(H):
            back = dot(square(wide1, h)[:E], head(ugrad, h), (0, 0))
            gq_ref[h * E : (h + 1) * E, :] = (query(h)[1] * back).astype(bf16)
        gq_out.start()

    all_total(
        at, pieces[1], wide2, near2, sent2, out2, half2, mine2, parts2, sems[12:], (lambda: None, query_grads)
    )

    grad_ref[...] = wide2[...].astype(bf16)
    res_out.wait()
    gq_out.wait()


def finish_kernel(
    first_ref, k_hbm, v_hbm, res_hbm, gq_hbm, grad_ref, clip_ref, flags_ref,
    res_out, gq_out, gk_out, gv_out,
    k, v, res, gq, gk, gv, loads, stores,
):
    tok = k.shape[1]
    pairs = [(k_hbm, k), (v_hbm, v), (res_hbm, res), (gq_hbm, gq)]
    incoming = [pltpu.make_async_copy(*pair, loads.at[i]) for i, pair in enumerate(pairs)]
    pairs = [(res, res_out), (gq, gq_out), (gk, gk_out), (gv, gv_out)]
    outgoing = [pltpu.make_async_copy(*pair, stores.at[i]) for i, pair in enumerate(pairs)]
    for load in incoming:
        load.start()
    valid = kept_tokens(tok, first_ref[0], clip_ref, flags_ref)
    incoming[0].wait()
    incoming[1].wait()
    for h in range(H):
        rows = slice(h * E, (h + 1) * E)
        total = grad_ref[:, rows]
        keys = k[rows, :].astype(f32)
        slope = jnp.where(keys > 0, 1.0, 0.0) * valid
        feat = (jnp.maximum(keys, 0.0) * valid).astype(bf16)
        gk[rows, :] = (slope * dot(total, v[rows, :], (0, 0))).astype(bf16)
        gv[rows, :] = dot(total, feat, (1, 0)).astype(bf16)
        if h == 1:
            for load, store in zip(incoming[2:], outgoing[:2]):
                load.wait()
                store.start()
    outgoing[2].start()
    outgoing[3].start()
    for store in outgoing:
        store.wait()


def local(
    query_rows,
    key_rows,
    value_rows,
    query_tangent,
    key_tangent,
    value_tangent,
    teacher,
    out_weight,
    norm_gain,
    clip_length,
    block_mask,
):
    tok, width = query_rows.shape
    depth = lax.axis_size("sub")
    chips = lax.axis_size("seq") // 2 * depth
    padded = -(-width // LANES) * LANES
    vmem = pltpu.VMEM
    dma = pltpu.SemaphoreType.DMA
    pieces = []
    totals = []
    for size in (2 * E, E):
        piece = -(-(size * padded // LANES) // (32 * chips)) * 16
        pieces.append(piece)
        half = (chips * piece, LANES)
        full = (2 * chips * piece, LANES)
        totals += [vmem((size, padded), f32), vmem(full, f32), vmem(full, bf16), vmem(full, bf16)]
        totals += [vmem(half, bf16)] * 3
    arrays = (query_rows, key_rows, value_rows, query_tangent, key_tangent, value_tangent)
    arrays = tuple(array.T for array in arrays + (teacher,)) + (out_weight,)
    anywhere = pl.BlockSpec(memory_space=pl.ANY)
    in_vmem = pl.BlockSpec(memory_space=vmem)
    in_smem = pl.BlockSpec(memory_space=pltpu.SMEM)
    wide_t = jax.ShapeDtypeStruct((width, tok), bf16)
    res_t = jax.ShapeDtypeStruct(teacher.shape[::-1], bf16)
    res, grad_query, grad = pl.pallas_call(
        functools.partial(step_kernel, chips, depth, pieces),
        out_shape=(res_t, wide_t, jax.ShapeDtypeStruct((E, padded), bf16)),
        in_specs=[anywhere] * 8 + [in_vmem, in_smem, in_smem],
        out_specs=[anywhere, anywhere, in_vmem],
        scratch_shapes=[vmem(array.shape, array.dtype) for array in arrays]
        + [dma((8,))]
        + totals
        + [
            vmem((width, tok), f32),
            vmem((H, 1, tok), f32),
            vmem((width, tok), bf16),
            vmem((width, tok), f32),
            vmem((width, tok), bf16),
            vmem(out_weight.shape[::-1], bf16),
            vmem((width, 1), f32),
            vmem(res_t.shape, bf16),
            vmem((width, tok), bf16),
            dma((2,)),
        ]
        + ([dma, dma] + [dma((chips,))] * 10) * 2,
        compiler_params=pltpu.CompilerParams(collective_id=0, has_side_effects=True),
    )(*arrays, norm_gain[None, :], clip_length, block_mask)
    first = (lax.axis_index("seq") * depth + lax.axis_index("sub")) * tok
    outs = pl.pallas_call(
        finish_kernel,
        out_shape=(res_t, wide_t, wide_t, wide_t),
        in_specs=[in_smem] + [anywhere] * 4 + [in_vmem, in_smem, in_smem],
        out_specs=[anywhere] * 4,
        scratch_shapes=[vmem(wide_t.shape, bf16)] * 2
        + [vmem(res_t.shape, bf16)]
        + [vmem(wide_t.shape, bf16)] * 3
        + [dma((4,)), dma((4,))],
    )(first[None], arrays[1], arrays[2], res, grad_query, grad, clip_length, block_mask)
    return tuple(out.T for out in outs)


def solution(mesh):
    return jax.shard_map(
        local,
        mesh=mesh,
        in_specs=(
            P(("seq", "sub"), None),
            P(("seq", "sub"), None),
            P(("seq", "sub"), None),
            P(("seq", "sub"), None),
            P(("seq", "sub"), None),
            P(("seq", "sub"), None),
            P(("seq", "sub"), None),
            P(),
            P(),
            P(),
            P(("seq", "sub")),
        ),
        out_specs=(
            P(("seq", "sub"), None),
            P(("seq", "sub"), None),
            P(("seq", "sub"), None),
            P(("seq", "sub"), None),
        ),
        check_vma=False,
    )
```
